32 devices in a mesh: scene: 2 (over y), tok: 8 (over z, x), hid: 2 (over core).
Axes of the slice: x: 2, y: 2, z: 4, core: 2. Of those that a mesh axis runs over, the one named last changes fastest.
Arguments:
- input_keys: bfloat16 [16384, 384], P(('scene', 'tok'), 'hid'), parts along dimension 0, may hold values from -6 to 6
- input_values: bfloat16 [16384, 384], P(('scene', 'tok'), 'hid'), parts along dimension 0, may hold values from -6 to 6
- input_lr: float32 [16384], P(('scene', 'tok')), parts along dimension 0, may hold values from 0.1 to 1
- gate_weight: bfloat16 [384, 1536], P('tok', 'hid'), may hold values from -0.3125 to 0.3125
- up_weight: bfloat16 [384, 1536], P('tok', 'hid'), may hold values from -0.3125 to 0.3125
- down_weight: bfloat16 [384, 1536], P('tok', 'hid'), may hold values from -0.15625 to 0.15625
- queries: bfloat16 [2048, 384], P(('scene', 'tok'), 'hid'), parts along dimension 0, may hold values from -6 to 6
- out_grad: bfloat16 [2048, 384], P(('scene', 'tok'), 'hid'), parts along dimension 0, may hold values from -6 to 6
Outputs:
- target_out: bfloat16 [2048, 384], P(('scene', 'tok'), 'hid'), parts along dimension 0
- query_grad: bfloat16 [2048, 384], P(('scene', 'tok'), 'hid'), parts along dimension 0
The draws below stay inside these ranges and needn't reach their ends.
There are 2 independent parts, one for each index of `scene`. The reference program is written for one: setup_inputs(seed, part) draws one part's arguments, and reference() takes and returns one part's arrays. A program takes and returns all parts, laid end to end along the dimension named above; an argument that names none is the same for every part. Nothing has to cross between parts.
All inputs are finite; a program needn't handle non-finite values.
Results may differ from the reference program's by a relative error of at most 0.009.
Values may be sent and summed in bfloat16 or wider, within the bound.
A program may use at most 64 MiB of HBM per device.

```python
import math
import jax
import jax.numpy as jnp
from jax import lax

D = 384
HID = 1536
TIN = 8192
TTG = 1024


def raised(drawn, stream_key, source, target, blocks, factor):
    def block_of(position):
        return (jnp.arange(drawn.shape[position]) // (drawn.shape[position] // blocks)).reshape((-1,) + (1,) * (drawn.ndim - 1 - position))

    near = jax.random.permutation(stream_key, blocks)[block_of(target)]
    far = (block_of(target) + blocks // 2) % blocks
    return jnp.where((block_of(source) == near) | (block_of(source) == far), factor * drawn, drawn)


def block_levels(own_key, shape, shards, low, high):
    def one(position, blocks):
        heights = jax.random.uniform(jax.random.fold_in(jax.random.fold_in(own_key, 6), position), (blocks,), jnp.float32, low / len(shards), high / len(shards))
        return jnp.repeat(jnp.exp(heights), shape[position] // blocks).reshape((-1,) + (1,) * (len(shape) - position - 1))

    loudness = one(*shards[0])
    for cut in shards[1:]:
        loudness = loudness * one(*cut)
    return loudness


def noise(rng, dims, scale, limit, cuts=(), held_as=jnp.bfloat16):
    drawn = scale * jax.random.normal(rng, dims, jnp.float32)
    if cuts:
        drawn = drawn * block_levels(rng, dims, cuts, -0.22, 0.18)
    return jnp.clip(drawn, -limit, limit).astype(held_as)


def bell_draw_with(own_key, extent, spread, reach, pieces, heavy, held_as=jnp.bfloat16):
    result = spread * jax.random.normal(own_key, extent, jnp.float32)
    if pieces:
        result = result * block_levels(own_key, extent, pieces, -0.22, 0.18)
    return jnp.clip(raised(result, jax.random.fold_in(own_key, 3), *heavy), -reach, reach).astype(held_as)


def setup_inputs(seed: int = 0, part: int = 0) -> dict:
    splits = jax.random.split(jax.random.key(seed), 9)
    part_keys = jax.random.split(jax.random.fold_in(splits[8], part), 9)
    return {
        "input_keys": bell_draw_with(part_keys[0], (TIN, D), 1.0, 6.0, ((0, 8), (1, 2)), (0, 1, 8, 2.0)),
        "input_values": bell_draw_with(part_keys[1], (TIN, D), 1.0, 6.0, ((0, 8), (1, 2)), (0, 1, 8, 2.0)),
        "input_lr": jnp.clip(jnp.exp(math.log(1.0) - 2.3025851 * jax.random.uniform(part_keys[2], (TIN,), jnp.float32) ** block_levels(part_keys[2], (TIN,), ((0, 8),), -0.2, 0.2)), 0.1, 1.0),
        "gate_weight": noise(splits[3], (D, HID), D ** -0.5, 0.3125, ((0, 8), (1, 2))),
        "up_weight": noise(splits[4], (D, HID), D ** -0.5, 0.3125, ((0, 8), (1, 2))),
        "down_weight": noise(splits[5], (D, HID), HID ** -0.5, 0.15625, ((0, 8), (1, 2))),
        "queries": noise(part_keys[6], (TTG, D), 1.0, 6.0, ((0, 8), (1, 2))),
        "out_grad": noise(part_keys[7], (TTG, D), 1.0, 6.0, ((0, 8), (1, 2))),
    }


step_ratio = 0.5
epsilon = 1e-06

def silu_slope(pre):
    sigma = jax.nn.sigmoid(pre)
    return sigma * (1.0 + pre * (1.0 - sigma))

def contract_rows(left, right):
    return lax.dot_general(left, right, (((0,), (0,)), ((), ())), preferred_element_type=jnp.float32)

def contract_cols(left, right):
    return lax.dot_general(left, right, (((1,), (1,)), ((), ())), preferred_element_type=jnp.float32)

def renew(weight, grad):
    base = weight.astype(jnp.float32)
    wsq = lax.optimization_barrier(jnp.sum(base * base, axis=1)) / HID
    gsq = lax.optimization_barrier(jnp.sum(grad * grad, axis=1)) / HID
    scale = step_ratio * jnp.sqrt(wsq) / jnp.sqrt(gsq + epsilon)
    moved = base - scale[:, None] * grad
    msq = lax.optimization_barrier(jnp.sum(moved * moved, axis=1)) / HID
    return (moved * (jnp.sqrt(wsq) / jnp.sqrt(msq + epsilon))[:, None]).astype(jnp.bfloat16)

def reference(input_keys, input_values, input_lr, gate_weight, up_weight, down_weight, queries, out_grad):
    total_in = input_keys.shape[0]
    block_in = min(total_in, 4096)
    count_in = total_in // block_in
    key_blocks = input_keys.reshape(count_in, block_in, D)
    value_blocks = input_values.reshape(count_in, block_in, D)
    rate_blocks = input_lr.reshape(count_in, block_in)

    def accumulate(carry, item):
        keys, values, rates = item
        scaled = (rates[:, None] * values.astype(jnp.float32)).astype(jnp.bfloat16)
        key_gate = jnp.dot(keys, gate_weight, preferred_element_type=jnp.float32)
        key_up = jnp.dot(keys, up_weight, preferred_element_type=jnp.float32)
        gate_act = jax.nn.silu(key_gate)
        key_act = (gate_act * key_up).astype(jnp.bfloat16)
        back = jnp.dot(scaled, down_weight, preferred_element_type=jnp.float32)
        d_gate = (-back * key_up * silu_slope(key_gate)).astype(jnp.bfloat16)
        d_up = (-back * gate_act).astype(jnp.bfloat16)
        grad_gate = carry[0] + contract_rows(keys, d_gate)
        grad_up = carry[1] + contract_rows(keys, d_up)
        grad_down = carry[2] - contract_rows(scaled, key_act)
        return ((grad_gate, grad_up, grad_down), None)
    zeros = jnp.zeros((D, HID), jnp.float32)
    (grad_gate, grad_up, grad_down), _ = lax.scan(accumulate, (zeros, zeros, zeros), (key_blocks, value_blocks, rate_blocks))
    new_gate = renew(gate_weight, grad_gate)
    new_up = renew(up_weight, grad_up)
    new_down = renew(down_weight, grad_down)
    total_tg = queries.shape[0]
    block_tg = min(total_tg, 4096)
    count_tg = total_tg // block_tg

    def apply_block(item):
        query_rows, grad_rows = item
        query_gate = jnp.dot(query_rows, new_gate, preferred_element_type=jnp.float32)
        query_up = jnp.dot(query_rows, new_up, preferred_element_type=jnp.float32)
        gate_act = jax.nn.silu(query_gate)
        query_act = (gate_act * query_up).astype(jnp.bfloat16)
        target_out = contract_cols(query_act, new_down).astype(jnp.bfloat16)
        query_back = jnp.dot(grad_rows, new_down, preferred_element_type=jnp.float32)
        q_gate_grad = (query_back * query_up * silu_slope(query_gate)).astype(jnp.bfloat16)
        q_up_grad = (query_back * gate_act).astype(jnp.bfloat16)
        query_grad = (contract_cols(q_gate_grad, new_gate) + contract_cols(q_up_grad, new_up)).astype(jnp.bfloat16)
        return (target_out, query_grad)
    outs_blocks, grad_blocks = lax.map(apply_block, (queries.reshape(count_tg, block_tg, D), out_grad.reshape(count_tg, block_tg, D)))
    return (outs_blocks.reshape(total_tg, D), grad_blocks.reshape(total_tg, D))
```

```python
import functools

import jax
import jax.numpy as jnp
from jax import lax
from jax.experimental import pallas as pl
from jax.experimental.pallas import tpu as pltpu
from jax.sharding import PartitionSpec as P

HID = 1536


step_ratio = 0.5
epsilon = 1e-06


def silu_slope(pre):
    sigma = jax.nn.sigmoid(pre)
    return sigma * (1.0 + pre * (1.0 - sigma))


def contract_rows(left, right):
    return lax.dot_general(
        left, right, (((0,), (0,)), ((), ())), preferred_element_type=jnp.float32
    )


def contract_cols(left, right):
    return lax.dot_general(
        left, right, (((1,), (1,)), ((), ())), preferred_element_type=jnp.float32
    )


def finish(moved, wsq, msq):
    return (moved * (jnp.sqrt(wsq) / jnp.sqrt(msq + epsilon))[:, None]).astype(jnp.bfloat16)


def shards_plain(
    input_keys, input_values, input_lr, gate_weight, up_weight, down_weight, queries, out_grad
):
    keys, values = (
        lax.all_gather(input_keys, "hid", axis=1, tiled=True),
        lax.all_gather(input_values, "hid", axis=1, tiled=True),
    )
    w_gate, w_up, w_down = (
        lax.all_gather(gate_weight, "tok", axis=0, tiled=True),
        lax.all_gather(up_weight, "tok", axis=0, tiled=True),
        lax.all_gather(down_weight, "tok", axis=0, tiled=True),
    )
    scaled = (input_lr[:, None] * values.astype(jnp.float32)).astype(jnp.bfloat16)
    key_gate = jnp.dot(keys, w_gate, preferred_element_type=jnp.float32)
    key_up = jnp.dot(keys, w_up, preferred_element_type=jnp.float32)
    gate_act = jax.nn.silu(key_gate)
    key_act = (gate_act * key_up).astype(jnp.bfloat16)
    back = jnp.dot(scaled, w_down, preferred_element_type=jnp.float32)
    d_gate = (-back * key_up * silu_slope(key_gate)).astype(jnp.bfloat16)
    d_up = (-back * gate_act).astype(jnp.bfloat16)
    width = gate_weight.shape[1]
    grads = lax.psum(
        jnp.concatenate(
            [
                contract_rows(keys, d_gate),
                contract_rows(keys, d_up),
                -contract_rows(scaled, key_act),
            ],
            axis=1,
        ),
        "tok",
    )
    olds = (w_gate, w_up, w_down)
    pieces = [grads[:, :width], grads[:, width : 2 * width], grads[:, 2 * width :]]
    weights = [old.astype(jnp.float32) for old in olds]
    renewed = []
    stats = []
    for weight, grad in zip(weights, pieces):
        stats.append(jnp.sum(weight * weight, axis=1))
        stats.append(jnp.sum(weight * grad, axis=1))
        stats.append(jnp.sum(grad * grad, axis=1))
    totals = lax.psum(
        (stats[0], stats[1], stats[2], stats[3], stats[4], stats[5], stats[6], stats[7], stats[8]),
        "hid",
    )
    for index in range(3):
        wsq = totals[3 * index] / HID
        cross = totals[3 * index + 1] / HID
        gsq = totals[3 * index + 2] / HID
        scale = step_ratio * jnp.sqrt(wsq) / jnp.sqrt(gsq + epsilon)
        moved = weights[index] - scale[:, None] * pieces[index]
        msq = wsq - 2.0 * scale * cross + scale * scale * gsq
        renewed.append(finish(moved, wsq, msq))
    new_gate, new_up, new_down = (renewed[0], renewed[1], renewed[2])
    query_rows, grad_rows = (
        lax.all_gather(queries, "hid", axis=1, tiled=True),
        lax.all_gather(out_grad, "hid", axis=1, tiled=True),
    )
    query_gate = jnp.dot(query_rows, new_gate, preferred_element_type=jnp.float32)
    query_up = jnp.dot(query_rows, new_up, preferred_element_type=jnp.float32)
    query_silu = jax.nn.silu(query_gate)
    query_act = (query_silu * query_up).astype(jnp.bfloat16)
    out_part = contract_cols(query_act, new_down)
    query_back = jnp.dot(grad_rows, new_down, preferred_element_type=jnp.float32)
    q_gate_grad = (query_back * query_up * silu_slope(query_gate)).astype(jnp.bfloat16)
    q_up_grad = (query_back * query_silu).astype(jnp.bfloat16)
    grad_part = contract_cols(q_gate_grad, new_gate) + contract_cols(q_up_grad, new_up)
    out_sum, grad_sum = (
        lax.psum_scatter(
            out_part.astype(jnp.bfloat16), "hid", scatter_dimension=1, tiled=True
        ).astype(jnp.float32),
        lax.psum_scatter(
            grad_part.astype(jnp.bfloat16), "hid", scatter_dimension=1, tiled=True
        ).astype(jnp.float32),
    )
    return (out_sum.astype(jnp.bfloat16), grad_sum.astype(jnp.bfloat16))


MESH = pl.DeviceIdType.MESH
WIDE = 2
ANY = pl.BlockSpec(memory_space=pl.ANY)
VM = pl.BlockSpec(memory_space=pltpu.VMEM)


def place(tok):
    rank = lax.axis_index("tok")
    return lax.div(rank, WIDE), lax.rem(rank, WIDE), tok // WIDE


def remote(src, dst, send, recv, **where):
    return pltpu.make_async_remote_copy(
        src_ref=src, dst_ref=dst, send_sem=send, recv_sem=recv,
        device_id=where, device_id_type=MESH,
    )


def greet(always, ends=()):
    barrier = pltpu.get_barrier_semaphore()

    def tell(where):
        pl.semaphore_signal(barrier, inc=1, device_id=where, device_id_type=MESH)

    for where in always:
        tell(where)
    for cond, where in ends:
        pl.when(cond)(functools.partial(tell, where))
    if not ends:
        pl.semaphore_wait(barrier, len(always))
        return
    both = ends[0][0] & ends[1][0]

    @pl.when(both)
    def _():
        pl.semaphore_wait(barrier, len(always) + 2)

    @pl.when(jnp.logical_not(both))
    def _():
        pl.semaphore_wait(barrier, len(always) + 1)


UP, DOWN, SIDE, OVER = range(4)


def spread_step(step, tok, active, own, out, send, recv, over):
    z, x, depth = place(tok)

    def pass_on(src, block, up, down):
        def go(cond, direction, **where):
            def start():
                remote(src, out.at[block], send.at[direction, block], recv.at[block], **where).start()
            if cond is None:
                start()
            else:
                pl.when(cond)(start)
        if up:
            go(z < depth - 1, UP, tok=(z + 1) * WIDE + x)
        if down:
            go(z > 0, DOWN, tok=(z - 1) * WIDE + x)
        go(None, SIDE, tok=z * WIDE + 1 - x)
        if over is not None and not (up and down):
            go(None, OVER, scene=over)

    def arrive(block):
        remote(out.at[block], out.at[block], send.at[0, block], recv.at[block], tok=block).wait_recv()

    def body():
        if step == 0:
            pass_on(own, z * WIDE + x, True, True)
            return

        @pl.when(z >= step)
        def _():
            block = (z - step) * WIDE + x
            arrive(block)
            pass_on(out.at[block], block, True, False)

        @pl.when(z + step < depth)
        def _():
            block = (z + step) * WIDE + x
            arrive(block)
            pass_on(out.at[block], block, False, True)

    if active is None:
        body()
    else:
        pl.when(active)(body)


def spread_side(tok, active, out, send, recv, over):
    z, x, depth = place(tok)

    def take(block):
        remote(out.at[block], out.at[block], send.at[0, block], recv.at[block], tok=block).wait_recv()
        if over is not None:
            remote(out.at[block], out.at[block], send.at[OVER, block], recv.at[block], scene=over).start()

    def body():
        take(z * WIDE + 1 - x)
        for step in range(1, depth):
            @pl.when(z >= step)
            def _():
                take((z - step) * WIDE + 1 - x)

            @pl.when(z + step < depth)
            def _():
                take((z + step) * WIDE + 1 - x)

    if active is None:
        body()
    else:
        pl.when(active)(body)


def spread_end(tok, active, out, send, recv, over):
    z, x, depth = place(tok)

    def sent(direction, block):
        remote(out.at[block], out.at[block], send.at[direction, block], recv.at[block], tok=block).wait_send()

    def body():
        for level in range(depth):
            block = level * WIDE + x
            sent(SIDE, block)

            @pl.when((z >= level) & (z < depth - 1))
            def _():
                sent(UP, block)

            @pl.when((z <= level) & (z > 0))
            def _():
                sent(DOWN, block)
            if over is not None:
                @pl.when(z != level)
                def _():
                    sent(OVER, block)
                sent(OVER, level * WIDE + 1 - x)

    if active is None:
        body()
    else:
        pl.when(active)(body)
    if over is not None:
        @pl.when(jnp.logical_not(active))
        def _():
            for step in range(tok):
                @pl.when(z * WIDE + x != step)
                def _():
                    remote(out.at[step], out.at[step], send.at[0, step], recv.at[step], tok=step).wait_recv()


def gather_kernel(tok, *refs):
    rows_in, weights_in, rows_out, weights_out = refs[:4], refs[4:7], refs[7:11], refs[11:14]
    pair_send, pair_recv, send, recv, local = refs[14:]
    z, x, depth = place(tok)
    scene = lax.axis_index("scene")
    core = lax.axis_index("hid")
    greet(
        ({"hid": 1 - core}, {"scene": 1 - scene}, {"tok": z * WIDE + 1 - x}),
        ((z < depth - 1, {"tok": (z + 1) * WIDE + x}), (z > 0, {"tok": (z - 1) * WIDE + x})),
    )
    plan = []
    for index in range(3):
        active = None if index == 2 else scene == index
        over = None if index == 2 else 1 - scene
        plan.append((active, weights_out[index], send.at[index], recv.at[index], over))
    for index, (active, out, s, r, over) in enumerate(plan):
        spread_step(0, tok, active, weights_in[index], out, s, r, over)
    pairs = []
    for index in range(4):
        pairs.append(remote(rows_in[index], rows_out[index], pair_send.at[index], pair_recv.at[index], hid=1 - core))
        pairs[-1].start()
    copies = []
    for index in range(3):
        copies.append(pltpu.make_async_copy(weights_in[index], weights_out[index].at[z * WIDE + x], local.at[index]))
        copies[-1].start()
    for step in range(1, depth):
        for index, (active, out, s, r, over) in enumerate(plan):
            spread_step(step, tok, active, weights_in[index], out, s, r, over)
    for active, out, s, r, over in plan:
        spread_side(tok, active, out, s, r, over)
    for active, out, s, r, over in plan:
        spread_end(tok, active, out, s, r, over)
    for copy in copies:
        copy.wait()
    for copy in pairs:
        copy.wait()


def gather(tok, rows, weights):
    return pl.pallas_call(
        functools.partial(gather_kernel, tok),
        out_shape=[jax.ShapeDtypeStruct(a.shape, a.dtype) for a in rows]
        + [jax.ShapeDtypeStruct((tok,) + a.shape, a.dtype) for a in weights],
        in_specs=[ANY] * 7,
        out_specs=[ANY] * 7,
        scratch_shapes=[
            pltpu.SemaphoreType.DMA((4,)),
            pltpu.SemaphoreType.DMA((4,)),
            pltpu.SemaphoreType.DMA((3, 4, tok)),
            pltpu.SemaphoreType.DMA((3, tok)),
            pltpu.SemaphoreType.DMA((3,)),
        ],
        compiler_params=pltpu.CompilerParams(collective_id=0, has_side_effects=True),
    )(*rows, *weights)


def join(core, mine, other, full):
    half = mine.shape[1]

    @pl.when(core == 0)
    def _():
        full[:, :half] = mine[...]
        full[:, half:] = other[...]

    @pl.when(core != 0)
    def _():
        full[:, :half] = other[...]
        full[:, half:] = mine[...]


def learn_kernel(chunk, keys_a, keys_b, vals_a, vals_b, lr, gate, up, down, out, keys, vals, totals):
    core = lax.axis_index("hid")
    join(core, keys_a, keys_b, keys)
    join(core, vals_a, vals_b, vals)
    totals[...] = jnp.zeros_like(totals)

    def body(step, carry):
        rows = pl.ds(pl.multiple_of(step * chunk, chunk), chunk)
        k = keys[rows, :]
        scaled = (lr[rows, :] * vals[rows, :].astype(jnp.float32)).astype(jnp.bfloat16)
        key_gate = jnp.dot(k, gate[...], preferred_element_type=jnp.float32)
        key_up = jnp.dot(k, up[...], preferred_element_type=jnp.float32)
        back = jnp.dot(scaled, down[...], preferred_element_type=jnp.float32)
        sigma = jax.nn.sigmoid(key_gate)
        act = key_gate * sigma
        key_act = (act * key_up).astype(jnp.bfloat16)
        d_gate = (-back * key_up * (sigma * (1.0 + key_gate * (1.0 - sigma)))).astype(jnp.bfloat16)
        d_up = (-back * act).astype(jnp.bfloat16)
        totals[0] += contract_rows(k, d_gate)
        totals[1] += contract_rows(k, d_up)
        totals[2] -= contract_rows(scaled, key_act)
        return carry

    lax.fori_loop(0, keys.shape[0] // chunk, body, 0)
    out[...] = totals[...].astype(out.dtype)


def learn(keys_a, keys_b, vals_a, vals_b, lr, gate, up, down):
    tokens, half = keys_a.shape
    width = gate.shape[1]
    return pl.pallas_call(
        functools.partial(learn_kernel, 256),
        out_shape=jax.ShapeDtypeStruct((3, 2 * half, width), jnp.bfloat16),
        in_specs=[VM] * 8,
        out_specs=VM,
        scratch_shapes=[
            pltpu.VMEM((tokens, 2 * half), jnp.bfloat16),
            pltpu.VMEM((tokens, 2 * half), jnp.bfloat16),
            pltpu.VMEM((3, 2 * half, width), jnp.float32),
        ],
    )(keys_a, keys_b, vals_a, vals_b, lr, gate, up, down)


def update_kernel(tok, hidden, grads, gate, up, down, out_gate, out_up, out_down,
                  from_side, to_z, from_z, total, stats, fresh,
                  side_send, side_recv, z_send, z_recv, pair_send, pair_recv, send, recv, local):
    z, x, depth = place(tok)
    core = lax.axis_index("hid")
    side = z * WIDE + 1 - x
    greet(
        ({"hid": 1 - core}, {"tok": side})
        + tuple({"tok": lax.rem(z + step, depth) * WIDE + x} for step in range(1, depth))
    )
    sides = []
    for step in range(1, depth + 1):
        level = lax.rem(z + step, depth)
        for index in range(3):
            sides.append(remote(grads.at[index, level * WIDE + 1 - x], from_side.at[step - 1, index],
                                side_send.at[step - 1, index], side_recv.at[step - 1, index], tok=side))
            sides[-1].start()
    alongs = []
    for step in range(1, depth + 1):
        level = lax.rem(z + step, depth)
        for index in range(3):
            sides[(step - 1) * 3 + index].wait_recv()
            both = grads[index, level * WIDE + x].astype(jnp.float32) + from_side[step - 1, index].astype(jnp.float32)
            if step == depth:
                total[index] = both
            else:
                to_z[step - 1, index] = both.astype(jnp.bfloat16)
                alongs.append(remote(to_z.at[step - 1, index], from_z.at[step - 1, index],
                                     z_send.at[step - 1, index], z_recv.at[step - 1, index], tok=level * WIDE + x))
                alongs[-1].start()
    olds = (gate, up, down)
    lanes = lax.broadcasted_iota(jnp.int32, stats.shape[1:], 1)
    table = jnp.zeros(stats.shape[1:], jnp.float32)
    for index in range(3):
        grad = total[index]
        for step in range(1, depth):
            alongs[(step - 1) * 3 + index].wait_recv()
            grad = grad + from_z[step - 1, index].astype(jnp.float32)
        total[index] = grad
        old = olds[index][...].astype(jnp.float32)
        for place_in, value in enumerate((old * old, old * grad, grad * grad)):
            table = jnp.where(lanes == 3 * index + place_in, jnp.sum(value, axis=1, keepdims=True), table)
    stats[0] = table
    swap = remote(stats.at[0], stats.at[1], pair_send, pair_recv, hid=1 - core)
    swap.start()
    swap.wait_recv()
    table = stats[0] + stats[1]
    outs = (out_gate, out_up, out_down)
    plan = [(outs[i], send.at[i], recv.at[i]) for i in range(3)]
    copies = []
    for index in range(3):
        wsq, cross, gsq = (
            jnp.sum(jnp.where(lanes == 3 * index + k, table, 0.0), axis=1, keepdims=True) / hidden for k in range(3)
        )
        scale = step_ratio * jnp.sqrt(wsq) / jnp.sqrt(gsq + epsilon)
        moved = olds[index][...].astype(jnp.float32) - scale * total[index]
        msq = wsq - 2.0 * scale * cross + scale * scale * gsq
        fresh[index] = (moved * (jnp.sqrt(wsq) / jnp.sqrt(msq + epsilon))).astype(jnp.bfloat16)
        out, s, r = plan[index]
        spread_step(0, tok, None, fresh.at[index], out, s, r, None)
        copies.append(pltpu.make_async_copy(fresh.at[index], out.at[z * WIDE + x], local.at[index]))
        copies[-1].start()
    for step in range(1, depth):
        for index, (out, s, r) in enumerate(plan):
            spread_step(step, tok, None, fresh.at[index], out, s, r, None)
    for out, s, r in plan:
        spread_side(tok, None, out, s, r, None)
    for out, s, r in plan:
        spread_end(tok, None, out, s, r, None)
    for copy in copies:
        copy.wait()
    for copy in sides + alongs + [swap]:
        copy.wait_send()


def update(tok, grads, gate, up, down):
    rows, width = gate.shape
    depth = tok // WIDE
    dma = pltpu.SemaphoreType.DMA
    blocks = (depth, 3, rows, width)
    return pl.pallas_call(
        functools.partial(update_kernel, tok, 2 * width),
        out_shape=[jax.ShapeDtypeStruct((tok, rows, width), jnp.bfloat16)] * 3,
        in_specs=[VM] * 4,
        out_specs=[ANY] * 3,
        scratch_shapes=[
            pltpu.VMEM(blocks, jnp.bfloat16),
            pltpu.VMEM(blocks, jnp.bfloat16),
            pltpu.VMEM(blocks, jnp.bfloat16),
            pltpu.VMEM((3, rows, width), jnp.float32),
            pltpu.VMEM((2, rows, 128), jnp.float32),
            pltpu.VMEM((3, rows, width), jnp.bfloat16),
            dma((depth, 3)), dma((depth, 3)), dma((depth, 3)), dma((depth, 3)),
            dma, dma,
            dma((3, 4, tok)), dma((3, tok)), dma((3,)),
        ],
        compiler_params=pltpu.CompilerParams(collective_id=1, has_side_effects=True),
    )(grads, gate, up, down)


def query_kernel(q_a, q_b, g_a, g_b, gate, up, down, mine, theirs, query_rows, grad_rows, parts, got, send, recv):
    core = lax.axis_index("hid")
    greet(({"hid": 1 - core},))
    join(core, q_a, q_b, query_rows)
    join(core, g_a, g_b, grad_rows)
    query_gate = jnp.dot(query_rows[...], gate[...], preferred_element_type=jnp.float32)
    query_up = jnp.dot(query_rows[...], up[...], preferred_element_type=jnp.float32)
    sigma = jax.nn.sigmoid(query_gate)
    query_silu = query_gate * sigma
    query_act = (query_silu * query_up).astype(jnp.bfloat16)
    half = q_a.shape[1]
    out_part = contract_cols(query_act, down[...])
    parts[0, 0] = out_part[:, :half].astype(jnp.bfloat16)
    parts[1, 0] = out_part[:, half:].astype(jnp.bfloat16)
    first = remote(parts.at[1 - core, 0], got.at[0], send.at[0], recv.at[0], hid=1 - core)
    first.start()
    query_back = jnp.dot(grad_rows[...], down[...], preferred_element_type=jnp.float32)
    q_gate_grad = (query_back * query_up * (sigma * (1.0 + query_gate * (1.0 - sigma)))).astype(jnp.bfloat16)
    q_up_grad = (query_back * query_silu).astype(jnp.bfloat16)
    grad_part = contract_cols(q_gate_grad, gate[...]) + contract_cols(q_up_grad, up[...])
    parts[0, 1] = grad_part[:, :half].astype(jnp.bfloat16)
    parts[1, 1] = grad_part[:, half:].astype(jnp.bfloat16)
    second = remote(parts.at[1 - core, 1], got.at[1], send.at[1], recv.at[1], hid=1 - core)
    second.start()
    mine[...] = parts[core]
    first.wait()
    second.wait()
    theirs[...] = got[...]


def query(q_a, q_b, g_a, g_b, gate, up, down):
    tokens, half = q_a.shape
    pair = jax.ShapeDtypeStruct((2, tokens, half), jnp.bfloat16)
    return pl.pallas_call(
        query_kernel,
        out_shape=[pair, pair],
        in_specs=[VM] * 7,
        out_specs=[VM] * 2,
        scratch_shapes=[
            pltpu.VMEM((tokens, 2 * half), jnp.bfloat16),
            pltpu.VMEM((tokens, 2 * half), jnp.bfloat16),
            pltpu.VMEM((2, 2, tokens, half), jnp.bfloat16),
            pltpu.VMEM((2, tokens, half), jnp.bfloat16),
            pltpu.SemaphoreType.DMA((2,)),
            pltpu.SemaphoreType.DMA((2,)),
        ],
        compiler_params=pltpu.CompilerParams(collective_id=2, has_side_effects=True),
    )(q_a, q_b, g_a, g_b, gate, up, down)


def shards_fast(
    tok, input_keys, input_values, input_lr, gate_weight, up_weight, down_weight, queries, out_grad
):
    rows, width = gate_weight.shape
    keys_b, vals_b, q_b, g_b, w_gate, w_up, w_down = gather(
        tok, (input_keys, input_values, queries, out_grad), (gate_weight, up_weight, down_weight)
    )
    flat = (tok * rows, width)
    grads = learn(
        input_keys, keys_b, input_values, vals_b, input_lr[:, None],
        w_gate.reshape(flat), w_up.reshape(flat), w_down.reshape(flat),
    )
    news = update(tok, grads.reshape(3, tok, rows, width), gate_weight, up_weight, down_weight)
    new_gate, new_up, new_down = (new.reshape(flat) for new in news)
    mine, theirs = query(queries, q_b, out_grad, g_b, new_gate, new_up, new_down)
    sums = [
        (mine[i].astype(jnp.float32) + theirs[i].astype(jnp.float32)).astype(jnp.bfloat16) for i in range(2)
    ]
    return (sums[0], sums[1])


def solution(mesh):
    tok = mesh.shape["tok"]
    fast = tok % WIDE == 0 and WIDE < tok <= 8 and mesh.shape["scene"] == 2 and mesh.shape["hid"] == 2
    shards = functools.partial(shards_fast, tok) if fast else shards_plain
    return jax.shard_map(
        shards,
        mesh=mesh,
        in_specs=(
            P(("scene", "tok"), "hid"),
            P(("scene", "tok"), "hid"),
            P(("scene", "tok")),
            P("tok", "hid"),
            P("tok", "hid"),
            P("tok", "hid"),
            P(("scene", "tok"), "hid"),
            P(("scene", "tok"), "hid"),
        ),
        out_specs=(P(("scene", "tok"), "hid"), P(("scene", "tok"), "hid")),
        check_vma=False,
    )
```

```python
import functools

import jax
import jax.numpy as jnp
from jax import lax
from jax.experimental import pallas as pl
from jax.experimental.pallas import tpu as pltpu
from jax.sharding import PartitionSpec as P

HID = 1536


step_ratio = 0.5
epsilon = 1e-06


def silu_slope(pre):
    sigma = jax.nn.sigmoid(pre)
    return sigma * (1.0 + pre * (1.0 - sigma))


def contract_rows(left, right):
    return lax.dot_general(
        left, right, (((0,), (0,)), ((), ())), preferred_element_type=jnp.float32
    )


def contract_cols(left, right):
    return lax.dot_general(
        left, right, (((1,), (1,)), ((), ())), preferred_element_type=jnp.float32
    )


def finish(moved, wsq, msq):
    return (moved * (jnp.sqrt(wsq) / jnp.sqrt(msq + epsilon))[:, None]).astype(jnp.bfloat16)


def shards_plain(
    input_keys, input_values, input_lr, gate_weight, up_weight, down_weight, queries, out_grad
):
    keys, values = (
        lax.all_gather(input_keys, "hid", axis=1, tiled=True),
        lax.all_gather(input_values, "hid", axis=1, tiled=True),
    )
    w_gate, w_up, w_down = (
        lax.all_gather(gate_weight, "tok", axis=0, tiled=True),
        lax.all_gather(up_weight, "tok", axis=0, tiled=True),
        lax.all_gather(down_weight, "tok", axis=0, tiled=True),
    )
    scaled = (input_lr[:, None] * values.astype(jnp.float32)).astype(jnp.bfloat16)
    key_gate = jnp.dot(keys, w_gate, preferred_element_type=jnp.float32)
    key_up = jnp.dot(keys, w_up, preferred_element_type=jnp.float32)
    gate_act = jax.nn.silu(key_gate)
    key_act = (gate_act * key_up).astype(jnp.bfloat16)
    back = jnp.dot(scaled, w_down, preferred_element_type=jnp.float32)
    d_gate = (-back * key_up * silu_slope(key_gate)).astype(jnp.bfloat16)
    d_up = (-back * gate_act).astype(jnp.bfloat16)
    width = gate_weight.shape[1]
    grads = lax.psum(
        jnp.concatenate(
            [
                contract_rows(keys, d_gate),
                contract_rows(keys, d_up),
                -contract_rows(scaled, key_act),
            ],
            axis=1,
        ),
        "tok",
    )
    olds = (w_gate, w_up, w_down)
    pieces = [grads[:, :width], grads[:, width : 2 * width], grads[:, 2 * width :]]
    weights = [old.astype(jnp.float32) for old in olds]
    renewed = []
    stats = []
    for weight, grad in zip(weights, pieces):
        stats.append(jnp.sum(weight * weight, axis=1))
        stats.append(jnp.sum(weight * grad, axis=1))
        stats.append(jnp.sum(grad * grad, axis=1))
    totals = lax.psum(
        (stats[0], stats[1], stats[2], stats[3], stats[4], stats[5], stats[6], stats[7], stats[8]),
        "hid",
    )
    for index in range(3):
        wsq = totals[3 * index] / HID
        cross = totals[3 * index + 1] / HID
        gsq = totals[3 * index + 2] / HID
        scale = step_ratio * jnp.sqrt(wsq) / jnp.sqrt(gsq + epsilon)
        moved = weights[index] - scale[:, None] * pieces[index]
        msq = wsq - 2.0 * scale * cross + scale * scale * gsq
        renewed.append(finish(moved, wsq, msq))
    new_gate, new_up, new_down = (renewed[0], renewed[1], renewed[2])
    query_rows, grad_rows = (
        lax.all_gather(queries, "hid", axis=1, tiled=True),
        lax.all_gather(out_grad, "hid", axis=1, tiled=True),
    )
    query_gate = jnp.dot(query_rows, new_gate, preferred_element_type=jnp.float32)
    query_up = jnp.dot(query_rows, new_up, preferred_element_type=jnp.float32)
    query_silu = jax.nn.silu(query_gate)
    query_act = (query_silu * query_up).astype(jnp.bfloat16)
    out_part = contract_cols(query_act, new_down)
    query_back = jnp.dot(grad_rows, new_down, preferred_element_type=jnp.float32)
    q_gate_grad = (query_back * query_up * silu_slope(query_gate)).astype(jnp.bfloat16)
    q_up_grad = (query_back * query_silu).astype(jnp.bfloat16)
    grad_part = contract_cols(q_gate_grad, new_gate) + contract_cols(q_up_grad, new_up)
    out_sum, grad_sum = (
        lax.psum_scatter(
            out_part.astype(jnp.bfloat16), "hid", scatter_dimension=1, tiled=True
        ).astype(jnp.float32),
        lax.psum_scatter(
            grad_part.astype(jnp.bfloat16), "hid", scatter_dimension=1, tiled=True
        ).astype(jnp.float32),
    )
    return (out_sum.astype(jnp.bfloat16), grad_sum.astype(jnp.bfloat16))


MESH = pl.DeviceIdType.MESH
WIDE = 2
ANY = pl.BlockSpec(memory_space=pl.ANY)
VM = pl.BlockSpec(memory_space=pltpu.VMEM)


def place(tok):
    rank = lax.axis_index("tok")
    return lax.div(rank, WIDE), lax.rem(rank, WIDE), tok // WIDE


def remote(src, dst, send, recv, **where):
    return pltpu.make_async_remote_copy(
        src_ref=src, dst_ref=dst, send_sem=send, recv_sem=recv,
        device_id=where, device_id_type=MESH,
    )


def greet(peers):
    barrier = pltpu.get_barrier_semaphore()
    for where in peers:
        pl.semaphore_signal(barrier, inc=1, device_id=where, device_id_type=MESH)
    pl.semaphore_wait(barrier, len(peers))


UP, DOWN, SIDE, OVER = range(4)


def spread_step(step, tok, active, own, out, send, recv, over):
    z, x, depth = place(tok)

    def pass_on(src, block, up, down):
        def go(cond, direction, **where):
            def start():
                remote(src, out.at[block], send.at[direction, block], recv.at[block], **where).start()
            if cond is None:
                start()
            else:
                pl.when(cond)(start)
        if up:
            go(z < depth - 1, UP, tok=(z + 1) * WIDE + x)
        if down:
            go(z > 0, DOWN, tok=(z - 1) * WIDE + x)
        go(None, SIDE, tok=z * WIDE + 1 - x)
        if over is not None and not (up and down):
            go(None, OVER, scene=over)

    def arrive(block):
        remote(out.at[block], out.at[block], send.at[0, block], recv.at[block], tok=block).wait_recv()

    def body():
        if step == 0:
            pass_on(own, z * WIDE + x, True, True)
            return

        @pl.when(z >= step)
        def _():
            block = (z - step) * WIDE + x
            arrive(block)
            pass_on(out.at[block], block, True, False)

        @pl.when(z + step < depth)
        def _():
            block = (z + step) * WIDE + x
            arrive(block)
            pass_on(out.at[block], block, False, True)

    if active is None:
        body()
    else:
        pl.when(active)(body)


def spread_side(tok, active, out, send, recv, over=None):
    z, x, depth = place(tok)

    def take(block):
        remote(out.at[block], out.at[block], send.at[0, block], recv.at[block], tok=block).wait_recv()
        if over is not None:
            remote(out.at[block], out.at[block], send.at[OVER, block], recv.at[block], scene=over).start()

    def body():
        take(z * WIDE + 1 - x)
        for step in range(1, depth):
            @pl.when(z >= step)
            def _():
                take((z - step) * WIDE + 1 - x)

            @pl.when(z + step < depth)
            def _():
                take((z + step) * WIDE + 1 - x)

    if active is None:
        body()
    else:
        pl.when(active)(body)


def spread_end(tok, active, out, send, recv, over):
    z, x, depth = place(tok)

    def sent(direction, block):
        remote(out.at[block], out.at[block], send.at[direction, block], recv.at[block], tok=block).wait_send()

    def body():
        for level in range(depth):
            block = level * WIDE + x
            sent(SIDE, block)

            @pl.when((z >= level) & (z < depth - 1))
            def _():
                sent(UP, block)

            @pl.when((z <= level) & (z > 0))
            def _():
                sent(DOWN, block)
            if over is not None:
                @pl.when(z != level)
                def _():
                    sent(OVER, block)
                sent(OVER, level * WIDE + 1 - x)

    if active is None:
        body()
    else:
        pl.when(active)(body)


def spread_over(tok, active, out, send, recv):
    z, x, depth = place(tok)

    @pl.when(jnp.logical_not(active))
    def _():
        for block in range(tok):
            @pl.when(z * WIDE + x != block)
            def _():
                remote(out.at[block], out.at[block], send.at[0, block], recv.at[block], tok=block).wait_recv()


def whole_kernel(
    tok, hidden, chunk,
    keys_in, vals_in, lr, q_in, g_in, gate_in, up_in, down_in,
    mine, theirs,
    keys, vals, q, g, olds, scaled, key_gate, key_up, key_act, d_gate, d_up,
    total, grads, from_side, to_z, from_z, stats, fresh, news, parts, got,
    pair_send, pair_recv, pair_local, old_send, old_recv, old_local,
    side_send, side_recv, z_send, z_recv, stat_send, stat_recv,
    new_send, new_recv, new_local, part_send, part_recv,
):
    z, x, depth = place(tok)
    scene = lax.axis_index("scene")
    core = lax.axis_index("hid")
    me = z * WIDE + x
    side = z * WIDE + 1 - x
    f32, bf16 = jnp.float32, jnp.bfloat16
    rows, width = gate_in.shape
    wide = tok * rows
    levels = [lax.rem(z + step, depth) for step in range(1, depth + 1)]
    greet(
        ({"hid": 1 - core}, {"scene": 1 - scene}, {"tok": side})
        + tuple({"tok": level * WIDE + x} for level in levels[:-1])
    )

    waits = []
    plan = []
    for index in range(3):
        active = None if index == 2 else scene == index
        over = None if index == 2 else 1 - scene
        plan.append((active, olds.at[index], old_send.at[index], old_recv.at[index], over))
    for index, own in enumerate((gate_in, up_in, down_in)):
        active, out, s, r, over = plan[index]
        spread_step(0, tok, active, own, out, s, r, over)
    copies = []
    pairs = []
    for index, (own, full) in enumerate(((keys_in, keys), (vals_in, vals), (q_in, q), (g_in, g))):
        pairs.append(remote(own, full.at[core], pair_send.at[index], pair_recv.at[index], hid=1 - core))
        pairs[-1].start()
        copies.append(pltpu.make_async_copy(own, full.at[core], pair_local.at[index]))
        copies[-1].start()
    for index, own in enumerate((gate_in, up_in, down_in)):
        copies.append(pltpu.make_async_copy(own, olds.at[index, me], old_local.at[index]))
        copies[-1].start()
    for step in range(1, depth):
        for active, out, s, r, over in plan:
            spread_step(step, tok, active, None, out, s, r, over)
    for active, out, s, r, over in plan[:2]:
        spread_side(tok, active, out, s, r, over)
    for active, out, s, r, over in plan[:2]:
        spread_over(tok, active, out, s, r)
    for copy in copies:
        copy.wait()
    for copy in pairs:
        copy.wait_recv()

    def forward(step, carry):
        at = pl.ds(pl.multiple_of(step * chunk, chunk), chunk)
        k = keys[:, :, at].reshape(wide, chunk)
        a = contract_rows(k, olds[0].reshape(wide, width))
        b = contract_rows(k, olds[1].reshape(wide, width))
        key_gate[at, :] = a
        key_up[at, :] = b
        key_act[at, :] = (a * jax.nn.sigmoid(a) * b).astype(bf16)
        v = vals[:, :, at].reshape(wide, chunk).astype(f32)
        scaled[:, at] = (lr[:, at] * v).astype(bf16)
        return carry

    def backward(step, carry):
        at = pl.ds(pl.multiple_of(step * chunk, chunk), chunk)
        back = contract_rows(scaled[:, at], olds[2].reshape(wide, width))
        a = key_gate[at, :]
        sigma = jax.nn.sigmoid(a)
        d_gate[at, :] = (-back * key_up[at, :] * (sigma * (1.0 + a * (1.0 - sigma)))).astype(bf16)
        d_up[at, :] = (-back * (a * sigma)).astype(bf16)
        return carry

    sides = {}
    alongs = {}
    swaps = {}

    def emit(index, grad):
        grad = grad.reshape(tok, rows, width)
        total[index] = grad
        grads[index] = grad.astype(bf16)
        for step, level in enumerate(levels):
            copy = remote(grads.at[index, level * WIDE + 1 - x], from_side.at[index, step],
                          side_send.at[index, step], side_recv.at[index, step], tok=side)
            copy.start()
            sides[index, step] = copy

    def relay(index):
        for step, level in enumerate(levels):
            sides[index, step].wait_recv()
            both = total[index, level * WIDE + x] + from_side[index, step].astype(f32)
            if step == depth - 1:
                total[index, me] = both
            else:
                to_z[index, step] = both.astype(bf16)
                copy = remote(to_z.at[index, step], from_z.at[index, step],
                              z_send.at[index, step], z_recv.at[index, step], tok=level * WIDE + x)
                copy.start()
                alongs[index, step] = copy

    lanes = lax.broadcasted_iota(jnp.int32, (rows, 128), 1)

    def measure(index):
        grad = total[index, me]
        for step in range(depth - 1):
            alongs[index, step].wait_recv()
            grad = grad + from_z[index, step].astype(f32)
        total[index, me] = grad
        old = olds[index, me].astype(f32)
        table = jnp.zeros((rows, 128), f32)
        for lane, value in enumerate((old * old, old * grad, grad * grad)):
            table = jnp.where(lanes == lane, jnp.sum(value, axis=1, keepdims=True), table)
        stats[index, 0] = table
        copy = remote(stats.at[index, 0], stats.at[index, 1], stat_send.at[index], stat_recv.at[index], hid=1 - core)
        copy.start()
        swaps[index] = copy

    renewed = [(None, news.at[i], new_send.at[i], new_recv.at[i], None) for i in range(3)]
    places = []

    def apply(index):
        swaps[index].wait_recv()
        table = (stats[index, 0] + stats[index, 1]) / hidden
        wsq, cross, gsq = (
            jnp.sum(jnp.where(lanes == lane, table, 0.0), axis=1, keepdims=True) for lane in range(3)
        )
        scale = step_ratio * jnp.sqrt(wsq) / jnp.sqrt(gsq + epsilon)
        moved = olds[index, me].astype(f32) - scale * total[index, me]
        msq = wsq - 2.0 * scale * cross + scale * scale * gsq
        fresh[index] = (moved * (jnp.sqrt(wsq) / jnp.sqrt(msq + epsilon))).astype(bf16)
        active, out, s, r, over = renewed[index]
        spread_step(0, tok, active, fresh.at[index], out, s, r, over)
        places.append(pltpu.make_async_copy(fresh.at[index], out.at[me], new_local.at[index]))
        places[-1].start()

    def pass_new(step, index):
        active, out, s, r, over = renewed[index]
        spread_step(step, tok, active, None, out, s, r, over)

    steps = keys.shape[2] // chunk
    lax.fori_loop(0, steps, forward, 0)
    emit(2, -jnp.dot(scaled[...], key_act[...], preferred_element_type=f32))
    spread_side(tok, *plan[2])
    lax.fori_loop(0, steps, backward, 0)
    all_keys = keys[...].reshape(wide, keys.shape[2])
    emit(0, jnp.dot(all_keys, d_gate[...], preferred_element_type=f32))
    relay(2)
    emit(1, jnp.dot(all_keys, d_up[...], preferred_element_type=f32))
    relay(0)
    measure(2)
    relay(1)
    apply(2)
    measure(0)
    apply(0)
    measure(1)
    apply(1)
    for step in range(1, depth):
        for index in (2, 0, 1):
            pass_new(step, index)

    def fetch(index):
        spread_side(tok, *renewed[index])
        places[(2, 0, 1).index(index)].wait()
        return news[index].reshape(wide, width)

    half, count = q.shape[1:]
    all_q = q[...].reshape(wide, count)
    all_g = g[...].reshape(wide, count)
    down = fetch(2)
    query_back = contract_rows(all_g, down)
    gate = fetch(0)
    query_gate = contract_rows(all_q, gate)
    sigma = jax.nn.sigmoid(query_gate)
    query_silu = query_gate * sigma
    q_up_grad = (query_back * query_silu).astype(bf16)
    up = fetch(1)
    query_up = contract_rows(all_q, up)

    def hand(index, part):
        parts[:, index] = part.reshape(2, half, count).astype(bf16)
        copy = remote(parts.at[1 - core, index], got.at[index], part_send.at[index], part_recv.at[index], hid=1 - core)
        copy.start()
        return copy

    first = hand(0, contract_cols(down, (query_silu * query_up).astype(bf16)))
    q_gate_grad = (query_back * query_up * (sigma * (1.0 + query_gate * (1.0 - sigma)))).astype(bf16)
    second = hand(1, contract_cols(gate, q_gate_grad) + contract_cols(up, q_up_grad))
    mine[...] = parts[core]
    for entry in plan + renewed:
        spread_end(tok, *entry)
    for copy in pairs + list(sides.values()) + list(alongs.values()) + list(swaps.values()):
        copy.wait_send()
    first.wait()
    second.wait()
    theirs[...] = got[...]


def shards_fast(
    tok, input_keys, input_values, input_lr, gate_weight, up_weight, down_weight, queries, out_grad
):
    rows, width = gate_weight.shape
    tokens, half = input_keys.shape
    count = queries.shape[0]
    depth = tok // WIDE
    f32, bf16, dma = jnp.float32, jnp.bfloat16, pltpu.SemaphoreType.DMA
    pair = jax.ShapeDtypeStruct((2, half, count), bf16)
    blocks = (3, tok, rows, width)
    along = (3, depth, rows, width)
    mine, theirs = pl.pallas_call(
        functools.partial(whole_kernel, tok, 2 * width, 256),
        out_shape=[pair, pair],
        in_specs=[ANY, ANY, VM, ANY, ANY, ANY, ANY, ANY],
        out_specs=[VM, VM],
        scratch_shapes=[
            pltpu.VMEM((2, half, tokens), bf16),
            pltpu.VMEM((2, half, tokens), bf16),
            pltpu.VMEM((2, half, count), bf16),
            pltpu.VMEM((2, half, count), bf16),
            pltpu.VMEM(blocks, bf16),
            pltpu.VMEM((2 * half, tokens), bf16),
            pltpu.VMEM((tokens, width), f32),
            pltpu.VMEM((tokens, width), f32),
            pltpu.VMEM((tokens, width), bf16),
            pltpu.VMEM((tokens, width), bf16),
            pltpu.VMEM((tokens, width), bf16),
            pltpu.VMEM(blocks, f32),
            pltpu.VMEM(blocks, bf16),
            pltpu.VMEM(along, bf16),
            pltpu.VMEM(along, bf16),
            pltpu.VMEM(along, bf16),
            pltpu.VMEM((3, 2, rows, 128), f32),
            pltpu.VMEM((3, rows, width), bf16),
            pltpu.VMEM(blocks, bf16),
            pltpu.VMEM((2, 2, half, count), bf16),
            pltpu.VMEM((2, half, count), bf16),
            dma((4,)), dma((4,)), dma((4,)),
            dma((3, 4, tok)), dma((3, tok)), dma((3,)),
            dma((3, depth)), dma((3, depth)), dma((3, depth)), dma((3, depth)),
            dma((3,)), dma((3,)),
            dma((3, 4, tok)), dma((3, tok)), dma((3,)),
            dma((2,)), dma((2,)),
        ],
        compiler_params=pltpu.CompilerParams(
            collective_id=0, has_side_effects=True, vmem_limit_bytes=50 * 1024 * 1024
        ),
    )(
        input_keys.T, input_values.T, input_lr.reshape(1, tokens), queries.T, out_grad.T,
        gate_weight, up_weight, down_weight,
    )
    sums = [
        (mine[i].astype(f32) + theirs[i].astype(f32)).astype(bf16).T for i in range(2)
    ]
    return (sums[0], sums[1])


def solution(mesh):
    tok = mesh.shape["tok"]
    fast = tok % WIDE == 0 and WIDE < tok <= 8 and mesh.shape["scene"] == 2 and mesh.shape["hid"] == 2
    shards = functools.partial(shards_fast, tok) if fast else shards_plain
    return jax.shard_map(
        shards,
        mesh=mesh,
        in_specs=(
            P(("scene", "tok"), "hid"),
            P(("scene", "tok"), "hid"),
            P(("scene", "tok")),
            P("tok", "hid"),
            P("tok", "hid"),
            P("tok", "hid"),
            P(("scene", "tok"), "hid"),
            P(("scene", "tok"), "hid"),
        ),
        out_specs=(P(("scene", "tok"), "hid"), P(("scene", "tok"), "hid")),
        check_vma=False,
    )
```

```python
import functools

import jax
import jax.numpy as jnp
from jax import lax
from jax.experimental import pallas as pl
from jax.experimental.pallas import tpu as pltpu
from jax.sharding import PartitionSpec as P

HID = 1536


step_ratio = 0.5
epsilon = 1e-06


def silu_slope(pre):
    sigma = jax.nn.sigmoid(pre)
    return sigma * (1.0 + pre * (1.0 - sigma))


def contract_rows(left, right):
    return lax.dot_general(
        left, right, (((0,), (0,)), ((), ())), preferred_element_type=jnp.float32
    )


def contract_cols(left, right):
    return lax.dot_general(
        left, right, (((1,), (1,)), ((), ())), preferred_element_type=jnp.float32
    )


def finish(moved, wsq, msq):
    return (moved * (jnp.sqrt(wsq) / jnp.sqrt(msq + epsilon))[:, None]).astype(jnp.bfloat16)


def shards_plain(
    input_keys, input_values, input_lr, gate_weight, up_weight, down_weight, queries, out_grad
):
    keys, values = (
        lax.all_gather(input_keys, "hid", axis=1, tiled=True),
        lax.all_gather(input_values, "hid", axis=1, tiled=True),
    )
    w_gate, w_up, w_down = (
        lax.all_gather(gate_weight, "tok", axis=0, tiled=True),
        lax.all_gather(up_weight, "tok", axis=0, tiled=True),
        lax.all_gather(down_weight, "tok", axis=0, tiled=True),
    )
    scaled = (input_lr[:, None] * values.astype(jnp.float32)).astype(jnp.bfloat16)
    key_gate = jnp.dot(keys, w_gate, preferred_element_type=jnp.float32)
    key_up = jnp.dot(keys, w_up, preferred_element_type=jnp.float32)
    gate_act = jax.nn.silu(key_gate)
    key_act = (gate_act * key_up).astype(jnp.bfloat16)
    back = jnp.dot(scaled, w_down, preferred_element_type=jnp.float32)
    d_gate = (-back * key_up * silu_slope(key_gate)).astype(jnp.bfloat16)
    d_up = (-back * gate_act).astype(jnp.bfloat16)
    width = gate_weight.shape[1]
    grads = lax.psum(
        jnp.concatenate(
            [
                contract_rows(keys, d_gate),
                contract_rows(keys, d_up),
                -contract_rows(scaled, key_act),
            ],
            axis=1,
        ),
        "tok",
    )
    olds = (w_gate, w_up, w_down)
    pieces = [grads[:, :width], grads[:, width : 2 * width], grads[:, 2 * width :]]
    weights = [old.astype(jnp.float32) for old in olds]
    renewed = []
    stats = []
    for weight, grad in zip(weights, pieces):
        stats.append(jnp.sum(weight * weight, axis=1))
        stats.append(jnp.sum(weight * grad, axis=1))
        stats.append(jnp.sum(grad * grad, axis=1))
    totals = lax.psum(
        (stats[0], stats[1], stats[2], stats[3], stats[4], stats[5], stats[6], stats[7], stats[8]),
        "hid",
    )
    for index in range(3):
        wsq = totals[3 * index] / HID
        cross = totals[3 * index + 1] / HID
        gsq = totals[3 * index + 2] / HID
        scale = step_ratio * jnp.sqrt(wsq) / jnp.sqrt(gsq + epsilon)
        moved = weights[index] - scale[:, None] * pieces[index]
        msq = wsq - 2.0 * scale * cross + scale * scale * gsq
        renewed.append(finish(moved, wsq, msq))
    new_gate, new_up, new_down = (renewed[0], renewed[1], renewed[2])
    query_rows, grad_rows = (
        lax.all_gather(queries, "hid", axis=1, tiled=True),
        lax.all_gather(out_grad, "hid", axis=1, tiled=True),
    )
    query_gate = jnp.dot(query_rows, new_gate, preferred_element_type=jnp.float32)
    query_up = jnp.dot(query_rows, new_up, preferred_element_type=jnp.float32)
    query_silu = jax.nn.silu(query_gate)
    query_act = (query_silu * query_up).astype(jnp.bfloat16)
    out_part = contract_cols(query_act, new_down)
    query_back = jnp.dot(grad_rows, new_down, preferred_element_type=jnp.float32)
    q_gate_grad = (query_back * query_up * silu_slope(query_gate)).astype(jnp.bfloat16)
    q_up_grad = (query_back * query_silu).astype(jnp.bfloat16)
    grad_part = contract_cols(q_gate_grad, new_gate) + contract_cols(q_up_grad, new_up)
    out_sum, grad_sum = (
        lax.psum_scatter(
            out_part.astype(jnp.bfloat16), "hid", scatter_dimension=1, tiled=True
        ).astype(jnp.float32),
        lax.psum_scatter(
            grad_part.astype(jnp.bfloat16), "hid", scatter_dimension=1, tiled=True
        ).astype(jnp.float32),
    )
    return (out_sum.astype(jnp.bfloat16), grad_sum.astype(jnp.bfloat16))


MESH = pl.DeviceIdType.MESH
WIDE = 2
HBM = pl.BlockSpec(memory_space=pltpu.HBM)
VM = pl.BlockSpec(memory_space=pltpu.VMEM)


def place(tok):
    rank = lax.axis_index("tok")
    return lax.div(rank, WIDE), lax.rem(rank, WIDE), tok // WIDE


def remote(src, dst, send, recv, **where):
    return pltpu.make_async_remote_copy(
        src_ref=src, dst_ref=dst, send_sem=send, recv_sem=recv,
        device_id=where, device_id_type=MESH,
    )


def greet(peers):
    barrier = pltpu.get_barrier_semaphore()
    for where in peers:
        pl.semaphore_signal(barrier, inc=1, device_id=where, device_id_type=MESH)
    pl.semaphore_wait(barrier, len(peers))


UP, DOWN, SIDE, OVER = range(4)


def spread_step(step, tok, active, own, out, send, recv, over):
    z, x, depth = place(tok)

    def pass_on(src, block, up, down):
        def go(cond, direction, **where):
            def start():
                remote(src, out.at[block], send.at[direction, block], recv.at[block], **where).start()
            if cond is None:
                start()
            else:
                pl.when(cond)(start)
        if up:
            go(z < depth - 1, UP, tok=(z + 1) * WIDE + x)
        if down:
            go(z > 0, DOWN, tok=(z - 1) * WIDE + x)
        go(None, SIDE, tok=z * WIDE + 1 - x)
        if over is not None and not (up and down):
            go(None, OVER, scene=over)

    def arrive(block):
        remote(out.at[block], out.at[block], send.at[0, block], recv.at[block], tok=block).wait_recv()

    def body():
        if step == 0:
            pass_on(own, z * WIDE + x, True, True)
            return

        @pl.when(z >= step)
        def _():
            block = (z - step) * WIDE + x
            arrive(block)
            pass_on(out.at[block], block, True, False)

        @pl.when(z + step < depth)
        def _():
            block = (z + step) * WIDE + x
            arrive(block)
            pass_on(out.at[block], block, False, True)

    if active is None:
        body()
    else:
        pl.when(active)(body)


def spread_side(tok, active, out, send, recv, over=None):
    z, x, depth = place(tok)

    def take(block):
        remote(out.at[block], out.at[block], send.at[0, block], recv.at[block], tok=block).wait_recv()
        if over is not None:
            remote(out.at[block], out.at[block], send.at[OVER, block], recv.at[block], scene=over).start()

    def body():
        take(z * WIDE + 1 - x)
        for step in range(1, depth):
            @pl.when(z >= step)
            def _():
                take((z - step) * WIDE + 1 - x)

            @pl.when(z + step < depth)
            def _():
                take((z + step) * WIDE + 1 - x)

    if active is None:
        body()
    else:
        pl.when(active)(body)


def spread_end(tok, active, out, send, recv, over):
    z, x, depth = place(tok)

    def sent(direction, block):
        remote(out.at[block], out.at[block], send.at[direction, block], recv.at[block], tok=block).wait_send()

    def body():
        for level in range(depth):
            block = level * WIDE + x
            sent(SIDE, block)

            @pl.when((z >= level) & (z < depth - 1))
            def _():
                sent(UP, block)

            @pl.when((z <= level) & (z > 0))
            def _():
                sent(DOWN, block)
            if over is not None:
                @pl.when(z != level)
                def _():
                    sent(OVER, block)
                sent(OVER, level * WIDE + 1 - x)

    if active is None:
        body()
    else:
        pl.when(active)(body)


def spread_over(tok, active, out, send, recv):
    z, x, depth = place(tok)

    @pl.when(jnp.logical_not(active))
    def _():
        for block in range(tok):
            @pl.when(z * WIDE + x != block)
            def _():
                remote(out.at[block], out.at[block], send.at[0, block], recv.at[block], tok=block).wait_recv()


def whole_kernel(
    tok, hidden, chunk,
    keys_in, vals_in, lr, q_in, g_in, gate_in, up_in, down_in,
    mine, theirs,
    keys, vals, q, g, olds, scaled, key_gate, key_up, key_act, d_gate, d_up,
    total, grads, from_side, to_z, from_z, stats, fresh, news, parts, got,
    pair_send, pair_recv, pair_local, old_send, old_recv, old_local,
    side_send, side_recv, z_send, z_recv, stat_send, stat_recv,
    new_send, new_recv, new_local, part_send, part_recv,
):
    z, x, depth = place(tok)
    scene = lax.axis_index("scene")
    core = lax.axis_index("hid")
    me = z * WIDE + x
    side = z * WIDE + 1 - x
    f32, bf16 = jnp.float32, jnp.bfloat16
    rows, width = gate_in.shape
    wide = tok * rows
    levels = [lax.rem(z + step, depth) for step in range(1, depth + 1)]
    greet(
        ({"hid": 1 - core}, {"scene": 1 - scene}, {"tok": side})
        + tuple({"tok": level * WIDE + x} for level in levels[:-1])
    )

    waits = []
    plan = []
    for index in range(3):
        active = None if index == 2 else scene == index
        over = None if index == 2 else 1 - scene
        plan.append((active, olds.at[index], old_send.at[index], old_recv.at[index], over))
    for index, own in enumerate((gate_in, up_in, down_in)):
        active, out, s, r, over = plan[index]
        spread_step(0, tok, active, own, out, s, r, over)
    copies = []
    pairs = []
    for index, (own, full) in enumerate(((keys_in, keys), (vals_in, vals), (q_in, q), (g_in, g))):
        pairs.append(remote(own, full.at[core], pair_send.at[index], pair_recv.at[index], hid=1 - core))
        pairs[-1].start()
        copies.append(pltpu.make_async_copy(own, full.at[core], pair_local.at[index]))
        copies[-1].start()
    for index, own in enumerate((gate_in, up_in, down_in)):
        copies.append(pltpu.make_async_copy(own, olds.at[index, me], old_local.at[index]))
        copies[-1].start()
    for step in range(1, depth):
        for active, out, s, r, over in plan:
            spread_step(step, tok, active, None, out, s, r, over)
    for active, out, s, r, over in plan[:2]:
        spread_side(tok, active, out, s, r, over)
    for active, out, s, r, over in plan[:2]:
        spread_over(tok, active, out, s, r)
    for copy in copies:
        copy.wait()
    for copy in pairs:
        copy.wait_recv()

    def forward(step, carry):
        at = pl.ds(pl.multiple_of(step * chunk, chunk), chunk)
        k = keys[:, :, at].reshape(wide, chunk)
        a = contract_rows(k, olds[0].reshape(wide, width))
        b = contract_rows(k, olds[1].reshape(wide, width))
        key_gate[at, :] = a
        key_up[at, :] = b
        key_act[at, :] = (a * jax.nn.sigmoid(a) * b).astype(bf16)
        v = vals[:, :, at].reshape(wide, chunk).astype(f32)
        scaled[:, at] = (lr[:, at] * v).astype(bf16)
        return carry

    def backward(step, carry):
        at = pl.ds(pl.multiple_of(step * chunk, chunk), chunk)
        back = contract_rows(scaled[:, at], olds[2].reshape(wide, width))
        a = key_gate[at, :]
        sigma = jax.nn.sigmoid(a)
        d_gate[at, :] = (-back * key_up[at, :] * (sigma * (1.0 + a * (1.0 - sigma)))).astype(bf16)
        d_up[at, :] = (-back * (a * sigma)).astype(bf16)
        return carry

    sides = {}
    alongs = {}
    swaps = {}

    def emit(index, grad):
        grad = grad.reshape(tok, rows, width)
        total[index] = grad
        grads[index] = grad.astype(bf16)
        for step, level in enumerate(levels):
            copy = remote(grads.at[index, level * WIDE + 1 - x], from_side.at[index, step],
                          side_send.at[index, step], side_recv.at[index, step], tok=side)
            copy.start()
            sides[index, step] = copy

    def relay(index):
        for step, level in enumerate(levels):
            sides[index, step].wait_recv()
            both = total[index, level * WIDE + x] + from_side[index, step].astype(f32)
            if step == depth - 1:
                total[index, me] = both
            else:
                to_z[index, step] = both.astype(bf16)
                copy = remote(to_z.at[index, step], from_z.at[index, step],
                              z_send.at[index, step], z_recv.at[index, step], tok=level * WIDE + x)
                copy.start()
                alongs[index, step] = copy

    lanes = lax.broadcasted_iota(jnp.int32, (rows, 128), 1)

    def measure(index):
        grad = total[index, me]
        for step in range(depth - 1):
            alongs[index, step].wait_recv()
            grad = grad + from_z[index, step].astype(f32)
        total[index, me] = grad
        old = olds[index, me].astype(f32)
        table = jnp.zeros((rows, 128), f32)
        for lane, value in enumerate((old * old, old * grad, grad * grad)):
            table = jnp.where(lanes == lane, jnp.sum(value, axis=1, keepdims=True), table)
        stats[index, 0] = table
        copy = remote(stats.at[index, 0], stats.at[index, 1], stat_send.at[index], stat_recv.at[index], hid=1 - core)
        copy.start()
        swaps[index] = copy

    renewed = [(None, news.at[i], new_send.at[i], new_recv.at[i], None) for i in range(3)]
    places = []

    def apply(index):
        swaps[index].wait_recv()
        table = (stats[index, 0] + stats[index, 1]) / hidden
        wsq, cross, gsq = (
            jnp.sum(jnp.where(lanes == lane, table, 0.0), axis=1, keepdims=True) for lane in range(3)
        )
        scale = step_ratio * jnp.sqrt(wsq) / jnp.sqrt(gsq + epsilon)
        moved = olds[index, me].astype(f32) - scale * total[index, me]
        msq = wsq - 2.0 * scale * cross + scale * scale * gsq
        fresh[index] = (moved * (jnp.sqrt(wsq) / jnp.sqrt(msq + epsilon))).astype(bf16)
        active, out, s, r, over = renewed[index]
        spread_step(0, tok, active, fresh.at[index], out, s, r, over)
        places.append(pltpu.make_async_copy(fresh.at[index], out.at[me], new_local.at[index]))
        places[-1].start()

    def pass_new(step, index):
        active, out, s, r, over = renewed[index]
        spread_step(step, tok, active, None, out, s, r, over)

    steps = keys.shape[2] // chunk
    lax.fori_loop(0, steps, forward, 0)
    emit(2, -jnp.dot(scaled[...], key_act[...], preferred_element_type=f32))
    spread_side(tok, *plan[2])
    lax.fori_loop(0, steps, backward, 0)
    all_keys = keys[...].reshape(wide, keys.shape[2])
    emit(0, jnp.dot(all_keys, d_gate[...], preferred_element_type=f32))
    relay(2)
    emit(1, jnp.dot(all_keys, d_up[...], preferred_element_type=f32))
    relay(0)
    measure(2)
    relay(1)
    apply(2)
    measure(0)
    apply(0)
    measure(1)
    apply(1)
    for step in range(1, depth):
        for index in (2, 0, 1):
            pass_new(step, index)

    def fetch(index):
        spread_side(tok, *renewed[index])
        places[(2, 0, 1).index(index)].wait()
        return news[index].reshape(wide, width)

    half, count = q.shape[1:]
    all_q = q[...].reshape(wide, count)
    all_g = g[...].reshape(wide, count)
    down = fetch(2)
    query_back = contract_rows(all_g, down)
    gate = fetch(0)
    query_gate = contract_rows(all_q, gate)
    sigma = jax.nn.sigmoid(query_gate)
    query_silu = query_gate * sigma
    q_up_grad = (query_back * query_silu).astype(bf16)
    up = fetch(1)
    query_up = contract_rows(all_q, up)

    def hand(index, part):
        parts[:, index] = part.reshape(2, half, count).astype(bf16)
        copy = remote(parts.at[1 - core, index], got.at[index], part_send.at[index], part_recv.at[index], hid=1 - core)
        copy.start()
        return copy

    first = hand(0, contract_cols(down, (query_silu * query_up).astype(bf16)))
    q_gate_grad = (query_back * query_up * (sigma * (1.0 + query_gate * (1.0 - sigma)))).astype(bf16)
    second = hand(1, contract_cols(gate, q_gate_grad) + contract_cols(up, q_up_grad))
    mine[...] = parts[core]
    for entry in plan + renewed:
        spread_end(tok, *entry)
    for copy in pairs + list(sides.values()) + list(alongs.values()) + list(swaps.values()):
        copy.wait_send()
    first.wait()
    second.wait()
    theirs[...] = got[...]


def shards_fast(
    tok, input_keys, input_values, input_lr, gate_weight, up_weight, down_weight, queries, out_grad
):
    rows, width = gate_weight.shape
    tokens, half = input_keys.shape
    count = queries.shape[0]
    depth = tok // WIDE
    f32, bf16, dma = jnp.float32, jnp.bfloat16, pltpu.SemaphoreType.DMA
    pair = jax.ShapeDtypeStruct((2, half, count), bf16)
    blocks = (3, tok, rows, width)
    along = (3, depth, rows, width)
    mine, theirs = pl.pallas_call(
        functools.partial(whole_kernel, tok, 2 * width, 256),
        out_shape=[pair, pair],
        in_specs=[HBM, HBM, VM, HBM, HBM, HBM, HBM, HBM],
        out_specs=[VM, VM],
        scratch_shapes=[
            pltpu.VMEM((2, half, tokens), bf16),
            pltpu.VMEM((2, half, tokens), bf16),
            pltpu.VMEM((2, half, count), bf16),
            pltpu.VMEM((2, half, count), bf16),
            pltpu.VMEM(blocks, bf16),
            pltpu.VMEM((2 * half, tokens), bf16),
            pltpu.VMEM((tokens, width), f32),
            pltpu.VMEM((tokens, width), f32),
            pltpu.VMEM((tokens, width), bf16),
            pltpu.VMEM((tokens, width), bf16),
            pltpu.VMEM((tokens, width), bf16),
            pltpu.VMEM(blocks, f32),
            pltpu.VMEM(blocks, bf16),
            pltpu.VMEM(along, bf16),
            pltpu.VMEM(along, bf16),
            pltpu.VMEM(along, bf16),
            pltpu.VMEM((3, 2, rows, 128), f32),
            pltpu.VMEM((3, rows, width), bf16),
            pltpu.VMEM(blocks, bf16),
            pltpu.VMEM((2, 2, half, count), bf16),
            pltpu.VMEM((2, half, count), bf16),
            dma((4,)), dma((4,)), dma((4,)),
            dma((3, 4, tok)), dma((3, tok)), dma((3,)),
            dma((3, depth)), dma((3, depth)), dma((3, depth)), dma((3, depth)),
            dma((3,)), dma((3,)),
            dma((3, 4, tok)), dma((3, tok)), dma((3,)),
            dma((2,)), dma((2,)),
        ],
        compiler_params=pltpu.CompilerParams(
            collective_id=0, has_side_effects=True, vmem_limit_bytes=67_000_000
        ),
    )(
        input_keys.T, input_values.T, input_lr.reshape(1, tokens), queries.T, out_grad.T,
        gate_weight, up_weight, down_weight,
    )
    sums = [
        (mine[i].astype(f32) + theirs[i].astype(f32)).astype(bf16).T for i in range(2)
    ]
    return (sums[0], sums[1])


def solution(mesh):
    tok = mesh.shape["tok"]
    fast = tok % WIDE == 0 and WIDE < tok <= 8 and mesh.shape["scene"] == 2 and mesh.shape["hid"] == 2
    shards = functools.partial(shards_fast, tok) if fast else shards_plain
    return jax.shard_map(
        shards,
        mesh=mesh,
        in_specs=(
            P(("scene", "tok"), "hid"),
            P(("scene", "tok"), "hid"),
            P(("scene", "tok")),
            P("tok", "hid"),
            P("tok", "hid"),
            P("tok", "hid"),
            P(("scene", "tok"), "hid"),
            P(("scene", "tok"), "hid"),
        ),
        out_specs=(P(("scene", "tok"), "hid"), P(("scene", "tok"), "hid")),
        check_vma=False,
    )
```

```python
import functools

import jax
import jax.numpy as jnp
from jax import lax
from jax.experimental import pallas as pl
from jax.experimental.pallas import tpu as pltpu
from jax.sharding import PartitionSpec as P

HID = 1536


step_ratio = 0.5
epsilon = 1e-06


def silu_slope(pre):
    sigma = jax.nn.sigmoid(pre)
    return sigma * (1.0 + pre * (1.0 - sigma))


def contract_rows(left, right):
    return lax.dot_general(
        left, right, (((0,), (0,)), ((), ())), preferred_element_type=jnp.float32
    )


def contract_cols(left, right):
    return lax.dot_general(
        left, right, (((1,), (1,)), ((), ())), preferred_element_type=jnp.float32
    )


def finish(moved, wsq, msq):
    return (moved * (jnp.sqrt(wsq) / jnp.sqrt(msq + epsilon))[:, None]).astype(jnp.bfloat16)


def shards_plain(
    input_keys, input_values, input_lr, gate_weight, up_weight, down_weight, queries, out_grad
):
    keys, values = (
        lax.all_gather(input_keys, "hid", axis=1, tiled=True),
        lax.all_gather(input_values, "hid", axis=1, tiled=True),
    )
    w_gate, w_up, w_down = (
        lax.all_gather(gate_weight, "tok", axis=0, tiled=True),
        lax.all_gather(up_weight, "tok", axis=0, tiled=True),
        lax.all_gather(down_weight, "tok", axis=0, tiled=True),
    )
    scaled = (input_lr[:, None] * values.astype(jnp.float32)).astype(jnp.bfloat16)
    key_gate = jnp.dot(keys, w_gate, preferred_element_type=jnp.float32)
    key_up = jnp.dot(keys, w_up, preferred_element_type=jnp.float32)
    gate_act = jax.nn.silu(key_gate)
    key_act = (gate_act * key_up).astype(jnp.bfloat16)
    back = jnp.dot(scaled, w_down, preferred_element_type=jnp.float32)
    d_gate = (-back * key_up * silu_slope(key_gate)).astype(jnp.bfloat16)
    d_up = (-back * gate_act).astype(jnp.bfloat16)
    width = gate_weight.shape[1]
    grads = lax.psum(
        jnp.concatenate(
            [
                contract_rows(keys, d_gate),
                contract_rows(keys, d_up),
                -contract_rows(scaled, key_act),
            ],
            axis=1,
        ),
        "tok",
    )
    olds = (w_gate, w_up, w_down)
    pieces = [grads[:, :width], grads[:, width : 2 * width], grads[:, 2 * width :]]
    weights = [old.astype(jnp.float32) for old in olds]
    renewed = []
    stats = []
    for weight, grad in zip(weights, pieces):
        stats.append(jnp.sum(weight * weight, axis=1))
        stats.append(jnp.sum(weight * grad, axis=1))
        stats.append(jnp.sum(grad * grad, axis=1))
    totals = lax.psum(
        (stats[0], stats[1], stats[2], stats[3], stats[4], stats[5], stats[6], stats[7], stats[8]),
        "hid",
    )
    for index in range(3):
        wsq = totals[3 * index] / HID
        cross = totals[3 * index + 1] / HID
        gsq = totals[3 * index + 2] / HID
        scale = step_ratio * jnp.sqrt(wsq) / jnp.sqrt(gsq + epsilon)
        moved = weights[index] - scale[:, None] * pieces[index]
        msq = wsq - 2.0 * scale * cross + scale * scale * gsq
        renewed.append(finish(moved, wsq, msq))
    new_gate, new_up, new_down = (renewed[0], renewed[1], renewed[2])
    query_rows, grad_rows = (
        lax.all_gather(queries, "hid", axis=1, tiled=True),
        lax.all_gather(out_grad, "hid", axis=1, tiled=True),
    )
    query_gate = jnp.dot(query_rows, new_gate, preferred_element_type=jnp.float32)
    query_up = jnp.dot(query_rows, new_up, preferred_element_type=jnp.float32)
    query_silu = jax.nn.silu(query_gate)
    query_act = (query_silu * query_up).astype(jnp.bfloat16)
    out_part = contract_cols(query_act, new_down)
    query_back = jnp.dot(grad_rows, new_down, preferred_element_type=jnp.float32)
    q_gate_grad = (query_back * query_up * silu_slope(query_gate)).astype(jnp.bfloat16)
    q_up_grad = (query_back * query_silu).astype(jnp.bfloat16)
    grad_part = contract_cols(q_gate_grad, new_gate) + contract_cols(q_up_grad, new_up)
    out_sum, grad_sum = (
        lax.psum_scatter(
            out_part.astype(jnp.bfloat16), "hid", scatter_dimension=1, tiled=True
        ).astype(jnp.float32),
        lax.psum_scatter(
            grad_part.astype(jnp.bfloat16), "hid", scatter_dimension=1, tiled=True
        ).astype(jnp.float32),
    )
    return (out_sum.astype(jnp.bfloat16), grad_sum.astype(jnp.bfloat16))


MESH = pl.DeviceIdType.MESH
WIDE = 2
HBM = pl.BlockSpec(memory_space=pltpu.HBM)
VM = pl.BlockSpec(memory_space=pltpu.VMEM)


def place(tok):
    rank = lax.axis_index("tok")
    return lax.div(rank, WIDE), lax.rem(rank, WIDE), tok // WIDE


def remote(src, dst, send, recv, **where):
    return pltpu.make_async_remote_copy(
        src_ref=src, dst_ref=dst, send_sem=send, recv_sem=recv,
        device_id=where, device_id_type=MESH,
    )


def greet(peers):
    barrier = pltpu.get_barrier_semaphore()
    for where in peers:
        pl.semaphore_signal(barrier, inc=1, device_id=where, device_id_type=MESH)
    pl.semaphore_wait(barrier, len(peers))


UP, DOWN, SIDE, OVER = range(4)


def spread_step(step, tok, active, own, out, send, recv, over):
    z, x, depth = place(tok)

    def pass_on(src, block, up, down):
        def go(cond, direction, **where):
            def start():
                remote(src, out.at[block], send.at[direction, block], recv.at[block], **where).start()
            if cond is None:
                start()
            else:
                pl.when(cond)(start)
        if up:
            go(z < depth - 1, UP, tok=(z + 1) * WIDE + x)
        if down:
            go(z > 0, DOWN, tok=(z - 1) * WIDE + x)
        go(None, SIDE, tok=z * WIDE + 1 - x)
        if over is not None and not (up and down):
            go(None, OVER, scene=over)

    def arrive(block):
        remote(out.at[block], out.at[block], send.at[0, block], recv.at[block], tok=block).wait_recv()

    def body():
        if step == 0:
            pass_on(own, z * WIDE + x, True, True)
            return

        @pl.when(z >= step)
        def _():
            block = (z - step) * WIDE + x
            arrive(block)
            pass_on(out.at[block], block, True, False)

        @pl.when(z + step < depth)
        def _():
            block = (z + step) * WIDE + x
            arrive(block)
            pass_on(out.at[block], block, False, True)

    if active is None:
        body()
    else:
        pl.when(active)(body)


def spread_side(tok, active, out, send, recv, over=None):
    z, x, depth = place(tok)

    def take(block):
        remote(out.at[block], out.at[block], send.at[0, block], recv.at[block], tok=block).wait_recv()
        if over is not None:
            remote(out.at[block], out.at[block], send.at[OVER, block], recv.at[block], scene=over).start()

    def body():
        take(z * WIDE + 1 - x)
        for step in range(1, depth):
            @pl.when(z >= step)
            def _():
                take((z - step) * WIDE + 1 - x)

            @pl.when(z + step < depth)
            def _():
                take((z + step) * WIDE + 1 - x)

    if active is None:
        body()
    else:
        pl.when(active)(body)


def spread_end(tok, active, out, send, recv, over):
    z, x, depth = place(tok)

    def sent(direction, block):
        remote(out.at[block], out.at[block], send.at[direction, block], recv.at[block], tok=block).wait_send()

    def body():
        for level in range(depth):
            block = level * WIDE + x
            sent(SIDE, block)

            @pl.when((z >= level) & (z < depth - 1))
            def _():
                sent(UP, block)

            @pl.when((z <= level) & (z > 0))
            def _():
                sent(DOWN, block)
            if over is not None:
                @pl.when(z != level)
                def _():
                    sent(OVER, block)
                sent(OVER, level * WIDE + 1 - x)

    if active is None:
        body()
    else:
        pl.when(active)(body)


def spread_over(tok, active, out, send, recv):
    z, x, depth = place(tok)

    @pl.when(jnp.logical_not(active))
    def _():
        for block in range(tok):
            @pl.when(z * WIDE + x != block)
            def _():
                remote(out.at[block], out.at[block], send.at[0, block], recv.at[block], tok=block).wait_recv()


def whole_kernel(
    tok, hidden, chunk,
    keys_in, vals_in, lr, q_in, g_in, gate_in, up_in, down_in,
    mine, theirs,
    keys, vals, q, g, olds, scaled, key_gate, key_up, key_act, d_gate, d_up,
    total, grads, from_side, to_z, from_z, stats, fresh, news, parts, got,
    pair_send, pair_recv, pair_local, old_send, old_recv, old_local,
    side_send, side_recv, z_send, z_recv, stat_send, stat_recv,
    new_send, new_recv, new_local, part_send, part_recv,
):
    z, x, depth = place(tok)
    scene = lax.axis_index("scene")
    core = lax.axis_index("hid")
    me = z * WIDE + x
    side = z * WIDE + 1 - x
    f32, bf16 = jnp.float32, jnp.bfloat16
    rows, width = gate_in.shape
    wide = tok * rows
    levels = [lax.rem(z + step, depth) for step in range(1, depth + 1)]
    greet(
        ({"hid": 1 - core}, {"scene": 1 - scene}, {"tok": side})
        + tuple({"tok": level * WIDE + x} for level in levels[:-1])
    )

    waits = []
    plan = []
    for index in range(3):
        active = None if index == 2 else scene == index
        over = None if index == 2 else 1 - scene
        plan.append((active, olds.at[index], old_send.at[index], old_recv.at[index], over))
    for index, own in enumerate((gate_in, up_in, down_in)):
        active, out, s, r, over = plan[index]
        spread_step(0, tok, active, own, out, s, r, over)
    copies = []
    pairs = []
    for index, (own, full) in enumerate(((keys_in, keys), (vals_in, vals), (q_in, q), (g_in, g))):
        pairs.append(remote(own, full.at[core], pair_send.at[index], pair_recv.at[index], hid=1 - core))
        pairs[-1].start()
        copies.append(pltpu.make_async_copy(own, full.at[core], pair_local.at[index]))
        copies[-1].start()
    for index, own in enumerate((gate_in, up_in, down_in)):
        copies.append(pltpu.make_async_copy(own, olds.at[index, me], old_local.at[index]))
        copies[-1].start()
    for step in range(1, depth):
        for active, out, s, r, over in plan:
            spread_step(step, tok, active, None, out, s, r, over)
    for active, out, s, r, over in plan[:2]:
        spread_side(tok, active, out, s, r, over)
    for active, out, s, r, over in plan[:2]:
        spread_over(tok, active, out, s, r)
    for copy in copies:
        copy.wait()
    for copy in pairs:
        copy.wait_recv()

    def forward(step, carry):
        at = pl.ds(pl.multiple_of(step * chunk, chunk), chunk)
        k = keys[:, :, at].reshape(wide, chunk)
        a = contract_rows(k, olds[0].reshape(wide, width))
        b = contract_rows(k, olds[1].reshape(wide, width))
        key_gate[at, :] = a
        key_up[at, :] = b
        key_act[at, :] = (a * jax.nn.sigmoid(a) * b).astype(bf16)
        v = vals[:, :, at].reshape(wide, chunk).astype(f32)
        scaled[:, at] = (lr[:, at] * v).astype(bf16)
        return carry

    def backward(step, carry):
        at = pl.ds(pl.multiple_of(step * chunk, chunk), chunk)
        back = contract_rows(scaled[:, at], olds[2].reshape(wide, width))
        a = key_gate[at, :]
        sigma = jax.nn.sigmoid(a)
        d_gate[at, :] = (-back * key_up[at, :] * (sigma * (1.0 + a * (1.0 - sigma)))).astype(bf16)
        d_up[at, :] = (-back * (a * sigma)).astype(bf16)
        return carry

    sides = {}
    alongs = {}
    swaps = {}

    def emit(index, grad):
        grad = grad.reshape(tok, rows, width)
        total[index] = grad
        grads[index] = grad.astype(bf16)
        for step, level in enumerate(levels):
            copy = remote(grads.at[index, level * WIDE + 1 - x], from_side.at[index, step],
                          side_send.at[index, step], side_recv.at[index, step], tok=side)
            copy.start()
            sides[index, step] = copy

    def relay(index):
        for step, level in enumerate(levels):
            sides[index, step].wait_recv()
            both = total[index, level * WIDE + x] + from_side[index, step].astype(f32)
            if step == depth - 1:
                total[index, me] = both
            else:
                to_z[index, step] = both.astype(bf16)
                copy = remote(to_z.at[index, step], from_z.at[index, step],
                              z_send.at[index, step], z_recv.at[index, step], tok=level * WIDE + x)
                copy.start()
                alongs[index, step] = copy

    lanes = lax.broadcasted_iota(jnp.int32, (rows, 128), 1)

    def measure(index):
        grad = total[index, me]
        for step in range(depth - 1):
            alongs[index, step].wait_recv()
            grad = grad + from_z[index, step].astype(f32)
        total[index, me] = grad
        old = olds[index, me].astype(f32)
        table = jnp.zeros((rows, 128), f32)
        for lane, value in enumerate((old * old, old * grad, grad * grad)):
            table = jnp.where(lanes == lane, jnp.sum(value, axis=1, keepdims=True), table)
        stats[index, 0] = table
        copy = remote(stats.at[index, 0], stats.at[index, 1], stat_send.at[index], stat_recv.at[index], hid=1 - core)
        copy.start()
        swaps[index] = copy

    renewed = [(None, news.at[i], new_send.at[i], new_recv.at[i], None) for i in range(3)]
    places = []

    def apply(index):
        swaps[index].wait_recv()
        table = (stats[index, 0] + stats[index, 1]) / hidden
        wsq, cross, gsq = (
            jnp.sum(jnp.where(lanes == lane, table, 0.0), axis=1, keepdims=True) for lane in range(3)
        )
        scale = step_ratio * jnp.sqrt(wsq) / jnp.sqrt(gsq + epsilon)
        moved = olds[index, me].astype(f32) - scale * total[index, me]
        msq = wsq - 2.0 * scale * cross + scale * scale * gsq
        fresh[index] = (moved * (jnp.sqrt(wsq) / jnp.sqrt(msq + epsilon))).astype(bf16)
        active, out, s, r, over = renewed[index]
        spread_step(0, tok, active, fresh.at[index], out, s, r, over)
        places.append(pltpu.make_async_copy(fresh.at[index], out.at[me], new_local.at[index]))
        places[-1].start()

    def pass_new(step, index):
        active, out, s, r, over = renewed[index]
        spread_step(step, tok, active, None, out, s, r, over)

    steps = keys.shape[2] // chunk
    lax.fori_loop(0, steps, forward, 0)
    emit(2, -jnp.dot(scaled[...], key_act[...], preferred_element_type=f32))
    spread_side(tok, *plan[2])
    lax.fori_loop(0, steps, backward, 0)
    all_keys = keys[...].reshape(wide, keys.shape[2])
    emit(0, jnp.dot(all_keys, d_gate[...], preferred_element_type=f32))
    relay(2)
    emit(1, jnp.dot(all_keys, d_up[...], preferred_element_type=f32))
    relay(0)
    measure(2)
    relay(1)
    apply(2)
    measure(0)
    apply(0)
    pass_new(1, 2)
    measure(1)
    apply(1)
    for index in (2, 0, 1):
        for step in range(2 if index == 2 else 1, depth):
            pass_new(step, index)

    def fetch(index):
        spread_side(tok, *renewed[index])
        places[(2, 0, 1).index(index)].wait()
        return news[index].reshape(wide, width)

    half, count = q.shape[1:]
    all_q = q[...].reshape(wide, count)
    all_g = g[...].reshape(wide, count)
    down = fetch(2)
    query_back = contract_rows(all_g, down)
    gate = fetch(0)
    query_gate = contract_rows(all_q, gate)
    sigma = jax.nn.sigmoid(query_gate)
    query_silu = query_gate * sigma
    q_up_grad = (query_back * query_silu).astype(bf16)
    up = fetch(1)
    query_up = contract_rows(all_q, up)

    def hand(index, part):
        parts[:, index] = part.reshape(2, half, count).astype(bf16)
        copy = remote(parts.at[1 - core, index], got.at[index], part_send.at[index], part_recv.at[index], hid=1 - core)
        copy.start()
        return copy

    first = hand(0, contract_cols(down, (query_silu * query_up).astype(bf16)))
    q_gate_grad = (query_back * query_up * (sigma * (1.0 + query_gate * (1.0 - sigma)))).astype(bf16)
    second = hand(1, contract_cols(gate, q_gate_grad) + contract_cols(up, q_up_grad))
    mine[...] = parts[core]
    for entry in plan + renewed:
        spread_end(tok, *entry)
    for copy in pairs + list(sides.values()) + list(alongs.values()) + list(swaps.values()):
        copy.wait_send()
    first.wait()
    second.wait()
    theirs[...] = got[...]


def shards_fast(
    tok, input_keys, input_values, input_lr, gate_weight, up_weight, down_weight, queries, out_grad
):
    rows, width = gate_weight.shape
    tokens, half = input_keys.shape
    count = queries.shape[0]
    depth = tok // WIDE
    f32, bf16, dma = jnp.float32, jnp.bfloat16, pltpu.SemaphoreType.DMA
    pair = jax.ShapeDtypeStruct((2, half, count), bf16)
    blocks = (3, tok, rows, width)
    along = (3, depth, rows, width)
    mine, theirs = pl.pallas_call(
        functools.partial(whole_kernel, tok, 2 * width, 256),
        out_shape=[pair, pair],
        in_specs=[HBM, HBM, VM, HBM, HBM, HBM, HBM, HBM],
        out_specs=[VM, VM],
        scratch_shapes=[
            pltpu.VMEM((2, half, tokens), bf16),
            pltpu.VMEM((2, half, tokens), bf16),
            pltpu.VMEM((2, half, count), bf16),
            pltpu.VMEM((2, half, count), bf16),
            pltpu.VMEM(blocks, bf16),
            pltpu.VMEM((2 * half, tokens), bf16),
            pltpu.VMEM((tokens, width), f32),
            pltpu.VMEM((tokens, width), f32),
            pltpu.VMEM((tokens, width), bf16),
            pltpu.VMEM((tokens, width), bf16),
            pltpu.VMEM((tokens, width), bf16),
            pltpu.VMEM(blocks, f32),
            pltpu.VMEM(blocks, bf16),
            pltpu.VMEM(along, bf16),
            pltpu.VMEM(along, bf16),
            pltpu.VMEM(along, bf16),
            pltpu.VMEM((3, 2, rows, 128), f32),
            pltpu.VMEM((3, rows, width), bf16),
            pltpu.VMEM(blocks, bf16),
            pltpu.VMEM((2, 2, half, count), bf16),
            pltpu.VMEM((2, half, count), bf16),
            dma((4,)), dma((4,)), dma((4,)),
            dma((3, 4, tok)), dma((3, tok)), dma((3,)),
            dma((3, depth)), dma((3, depth)), dma((3, depth)), dma((3, depth)),
            dma((3,)), dma((3,)),
            dma((3, 4, tok)), dma((3, tok)), dma((3,)),
            dma((2,)), dma((2,)),
        ],
        compiler_params=pltpu.CompilerParams(
            collective_id=0, has_side_effects=True, vmem_limit_bytes=67_000_000
        ),
    )(
        input_keys.T, input_values.T, input_lr.reshape(1, tokens), queries.T, out_grad.T,
        gate_weight, up_weight, down_weight,
    )
    sums = [
        (mine[i].astype(f32) + theirs[i].astype(f32)).astype(bf16).T for i in range(2)
    ]
    return (sums[0], sums[1])


def solution(mesh):
    tok = mesh.shape["tok"]
    fast = tok % WIDE == 0 and WIDE < tok <= 8 and mesh.shape["scene"] == 2 and mesh.shape["hid"] == 2
    shards = functools.partial(shards_fast, tok) if fast else shards_plain
    return jax.shard_map(
        shards,
        mesh=mesh,
        in_specs=(
            P(("scene", "tok"), "hid"),
            P(("scene", "tok"), "hid"),
            P(("scene", "tok")),
            P("tok", "hid"),
            P("tok", "hid"),
            P("tok", "hid"),
            P(("scene", "tok"), "hid"),
            P(("scene", "tok"), "hid"),
        ),
        out_specs=(P(("scene", "tok"), "hid"), P(("scene", "tok"), "hid")),
        check_vma=False,
    )
```
